128 devices in a mesh: group: 8 (over x_lo, y), tp: 16 (over z, x_hi, core).
Axes of the slice: x: 4 (x_hi: 2, x_lo: 2; x = x_hi * 2 + x_lo), y: 4, z: 4, core: 2. Of those that a mesh axis runs over, the one named last changes fastest.
Arguments:
- weight_tiles: bfloat16 [8, 1792, 128, 128], P('group', 'tp'), may hold values from -0.0625 to 0.0625
- gradients: bfloat16 [8, 1792, 128, 128], P('group', 'tp'), may hold values from -6 to 6
- momentum: float32 [8, 1792, 128, 128], P('group', 'tp'), may hold values from -6 to 6
- slot_place: int32 [1792], replicated, may hold values from 0 to 111, as said below
- refresh: int32 [2], replicated, may hold values from 0 to 7, as said below
Outputs:
- slices: bfloat16 [8, 2, 2, 2048, 7168], P('group', None, None, 'tp')
- block_scales: bfloat16 [8, 2, 2, 16, 56], P('group', None, None, 'tp')
The draws below stay inside these ranges and needn't reach their ends.
Inputs may be any that keep to these rules, and one draw needn't show every extreme that they name: `slot_place`: for each tensor slice r, the slots s with (s mod (112)) // 7 == r hold every position 0 to 111 once. `refresh`: distinct expert ids.
All inputs are finite; a program needn't handle non-finite values.
Results may differ from the reference program's by a relative error of at most 0.009.
Values may be sent and summed in bfloat16 or wider, within the bound.
No kernel may reach another device: no remote copies, remote signals or barrier semaphores. Data moves between devices by JAX's collectives and lax.ppermute only.
A program may use at most 128 MiB of HBM per device.

```python
import jax
import jax.numpy as jnp

D = 7168
TILE = 128
REFRESH = 2
EXPERTS = 8
SLOT_K = 7
TILES = 1792
N_GROUP = 8
N_TP = 16


def draw_slot_place(key, part):
    keys = jax.random.split(jax.random.fold_in(key, 11), N_TP)
    orders = jax.vmap(lambda single: jax.random.permutation(single, N_TP * SLOT_K))(keys)
    orders = orders.reshape(N_TP, N_TP, SLOT_K).transpose(1, 0, 2)
    return orders.reshape(-1).astype(jnp.int32)


def draw_refresh(key, part):
    others = jax.random.permutation(jax.random.fold_in(key, 23), EXPERTS - 1)
    listed = jnp.concatenate([jnp.full((1,), EXPERTS - 1, jnp.int32), others[:REFRESH - 1].astype(jnp.int32)])
    shuffled = jax.random.permutation(jax.random.fold_in(key, 29), REFRESH)
    return listed[shuffled].astype(jnp.int32)


def block_scale(rng, dims, cuts, least, high):
    loudness, own = 1.0, jax.random.fold_in(rng, 6)
    for axis_at, blocks in cuts:
        heights = jnp.exp(jax.random.uniform(jax.random.fold_in(own, axis_at), (blocks,), jnp.float32, least / len(cuts), high / len(cuts)))
        loudness = loudness * jnp.repeat(heights, dims[axis_at] // blocks).reshape([-1 if axis == axis_at else 1 for axis in range(len(dims))])
    return loudness


def normal_values(key, dims, deviation, most, cuts=(), kind=jnp.bfloat16):
    drawn = deviation * jax.random.normal(key, dims, jnp.float32)
    if cuts:
        drawn = drawn * block_scale(key, dims, cuts, -0.22, 0.18)
    return jnp.clip(drawn, -most, most).astype(kind)


def setup_inputs(seed: int = 0) -> dict:
    seeds = jax.random.split(jax.random.key(seed), 6)
    weight_tiles = normal_values(seeds[0], (EXPERTS, TILES, TILE, TILE), D ** -0.5, 0.0625, ((0, 8), (1, 16)))
    gradients = normal_values(seeds[1], (EXPERTS, TILES, TILE, TILE), 1.0, 6.0, ((0, 8), (1, 16)))
    momentum = normal_values(seeds[2], (EXPERTS, TILES, TILE, TILE), 1.0, 6.0, ((0, 8), (1, 16)), jnp.float32)
    slot_place = draw_slot_place(jax.random.fold_in(seeds[5], 71), 0)
    refresh = draw_refresh(jax.random.fold_in(seeds[5], 71), 0)
    return dict(weight_tiles=weight_tiles, gradients=gradients, momentum=momentum, slot_place=slot_place, refresh=refresh)


learn_rate = 0.01
decay_rate = 0.1
momentum_decay = 0.9
epsilon = 1e-6
fp_range = 448.0


def updated_blocks(weight_tiles, gradients, momentum):
    updated = weight_tiles.astype(jnp.float32) * (1.0 - learn_rate * decay_rate) - learn_rate * (momentum_decay * momentum.astype(jnp.float32) + gradients.astype(jnp.float32))
    largest = jnp.max(jnp.abs(updated), axis=(2, 3))
    scales = ((largest + epsilon) / fp_range).astype(jnp.bfloat16)
    payload = (updated / scales.astype(jnp.float32)[:, :, None, None]).astype(jnp.bfloat16)
    return payload, scales


def arrange(payload, scales, positions):
    count = payload.shape[0]
    tile = payload.shape[2]
    columns = D // tile
    row_blocks = payload.shape[1] // columns
    ordering = jnp.argsort(positions).astype(jnp.int32)
    placed = jnp.take(payload, ordering, axis=1)
    placed = placed.reshape(count, row_blocks, columns, tile, tile).transpose(0, 1, 3, 2, 4)
    placed = placed.reshape(count, 2, row_blocks * tile // 2, columns * tile)
    scaled = jnp.take(scales, ordering, axis=1).reshape(count, 2, row_blocks // 2, columns)
    return placed, scaled


def reference(weight_tiles, gradients, momentum, slot_place, refresh):
    payload, scales = updated_blocks(weight_tiles[refresh], gradients[refresh], momentum[refresh])
    count = payload.shape[0]
    grid = slot_place.reshape(N_TP, N_TP, SLOT_K)
    blocks = payload.reshape(count, N_TP, N_TP, SLOT_K, TILE, TILE)
    scale_grid = scales.reshape(count, N_TP, N_TP, SLOT_K)
    pieces = []
    scale_pieces = []
    for slice_rank in range(N_TP):
        mine = grid[:, slice_rank].reshape(-1)
        placed, scaled = arrange(blocks[:, :, slice_rank].reshape(count, N_TP * SLOT_K, TILE, TILE), scale_grid[:, :, slice_rank].reshape(count, N_TP * SLOT_K), mine)
        pieces.append(placed)
        scale_pieces.append(scaled)
    whole = jnp.concatenate(pieces, axis=2)
    whole_scales = jnp.concatenate(scale_pieces, axis=2)
    return jnp.broadcast_to(whole[None], (N_GROUP,) + whole.shape), jnp.broadcast_to(whole_scales[None], (N_GROUP,) + whole_scales.shape)
```

```python
import functools

import jax
import jax.numpy as jnp
from jax import lax
from jax.experimental import pallas as pl
from jax.experimental.pallas import tpu as pltpu
from jax.sharding import PartitionSpec as P

D = 7168
TILE = 128
COLUMNS = D // TILE
SLOT_K = 7
N_GROUP = 8
N_TP = 16
BAND = TILE // N_GROUP
SCALE_ROWS = 8
ROWS = SLOT_K * BAND + SCALE_ROWS
PART = COLUMNS // 2 * TILE

learn_rate = 0.01
decay_rate = 0.1
momentum_decay = 0.9
epsilon = 1e-06
fp_range = 448.0

VMEM_LIMIT = 60 << 20


def step_kernel(w_ref, g_ref, m_ref, out_ref):
    for r in range(out_ref.shape[1]):
        tiles = pl.ds(r * SLOT_K, SLOT_K)
        updated = w_ref[tiles].astype(jnp.float32) * (1.0 - learn_rate * decay_rate) - learn_rate * (
            momentum_decay * m_ref[tiles] + g_ref[tiles].astype(jnp.float32)
        )
        largest = jnp.max(jnp.max(jnp.abs(updated), axis=1, keepdims=True), axis=2, keepdims=True)
        scale = ((largest + epsilon) / fp_range).astype(jnp.bfloat16)
        payload = (updated * (1.0 / scale.astype(jnp.float32))).astype(jnp.bfloat16)
        for k in range(SLOT_K):
            out_ref[:, r, k * BAND : (k + 1) * BAND, :] = payload[k].reshape(N_GROUP, BAND, TILE)
        row = lax.broadcasted_iota(jnp.int32, (SCALE_ROWS, TILE), 0)
        rows = jnp.zeros((SCALE_ROWS, TILE), jnp.float32)
        for k in range(SLOT_K):
            rows = jnp.where(row == k, jnp.broadcast_to(scale[k].astype(jnp.float32), rows.shape), rows)
        rows = rows.astype(jnp.bfloat16)
        for g in range(N_GROUP):
            out_ref[g, r, SLOT_K * BAND :, :] = rows


def step(weight_tiles, gradients, momentum, slices=2):
    tiles = slices * SLOT_K
    spec = pl.BlockSpec((tiles, TILE, TILE), lambda i: (i, 0, 0))
    return pl.pallas_call(
        step_kernel,
        grid=(N_TP // slices,),
        in_specs=[spec] * 3,
        out_specs=pl.BlockSpec((N_GROUP, slices, ROWS, TILE), lambda i: (0, i, 0, 0)),
        out_shape=jax.ShapeDtypeStruct((N_GROUP, N_TP, ROWS, TILE), jnp.bfloat16),
        compiler_params=pltpu.CompilerParams(vmem_limit_bytes=VMEM_LIMIT),
        name="step",
    )(weight_tiles, gradients, momentum)


def place_kernel(place_ref, refresh_ref, rank_ref, recv_ref, a_ref, b_ref, buf, placed, sem_in, sem_out):
    rank = rank_ref[0]
    fetch = [
        pltpu.make_async_copy(recv_ref.at[refresh_ref[j]], buf.at[j], sem_in.at[j])
        for j in range(2)
    ]
    for copy in fetch:
        copy.start()
    store = []
    for j in range(2):
        fetch[j].wait()

        def owner(t, _, j=j):
            for k in range(SLOT_K):
                p = place_ref[t * (N_TP * SLOT_K) + rank * SLOT_K + k]
                half = (p >= COLUMNS).astype(jnp.int32)
                column = pl.multiple_of((p - COLUMNS * half) * TILE, TILE)
                placed[j, half, :, pl.ds(column, TILE)] = buf[j, t, k * BAND : (k + 1) * BAND, :]
            return 0

        lax.fori_loop(0, N_TP, owner, 0)
        for side, ref in enumerate((a_ref, b_ref)):
            copy = pltpu.make_async_copy(
                placed.at[j, :, :, pl.ds(side * PART, PART)], ref.at[j], sem_out.at[j, side]
            )
            copy.start()
            store.append(copy)
    for copy in store:
        copy.wait()


def place(slot_place, refresh, rank, recv):
    part = jax.ShapeDtypeStruct((2, 2, BAND, PART), jnp.bfloat16)
    smem = pl.BlockSpec(memory_space=pltpu.SMEM)
    return pl.pallas_call(
        place_kernel,
        in_specs=[smem, smem, smem, pl.BlockSpec(memory_space=pl.ANY)],
        out_specs=[pl.BlockSpec(memory_space=pl.ANY)] * 2,
        out_shape=[part, part],
        scratch_shapes=[
            pltpu.VMEM((2, N_TP, ROWS, TILE), jnp.bfloat16),
            pltpu.VMEM((2, 2, BAND, D), jnp.bfloat16),
            pltpu.SemaphoreType.DMA((2,)),
            pltpu.SemaphoreType.DMA((2, 2)),
        ],
        compiler_params=pltpu.CompilerParams(vmem_limit_bytes=VMEM_LIMIT),
        name="place",
    )(slot_place, refresh, rank, recv)


def scales_kernel(place_ref, refresh_ref, rank_ref, recv_ref, out_ref, buf, sem):
    rank = rank_ref[0]
    fetch = [
        pltpu.make_async_copy(
            recv_ref.at[refresh_ref[j], :, pl.ds(SLOT_K * BAND, SCALE_ROWS), :], buf.at[j], sem.at[j]
        )
        for j in range(2)
    ]
    for copy in fetch:
        copy.start()
    at = lax.broadcasted_iota(jnp.int32, (SCALE_ROWS, TILE), 0) * TILE + lax.broadcasted_iota(
        jnp.int32, (SCALE_ROWS, TILE), 1
    )
    for j in range(2):
        fetch[j].wait()

        def owner(t, halves, j=j):
            rows = buf[j, t].astype(jnp.float32)
            first, second = halves
            for k in range(SLOT_K):
                p = place_ref[t * (N_TP * SLOT_K) + rank * SLOT_K + k]
                first = jnp.where(at == k * TILE + p, rows, first)
                second = jnp.where(at == k * TILE + p - COLUMNS, rows, second)
            return first, second

        empty = jnp.zeros((SCALE_ROWS, TILE), jnp.float32)
        for half, found in enumerate(lax.fori_loop(0, N_TP, owner, (empty, empty))):
            total = jnp.sum(found, axis=0, keepdims=True)
            out_ref[j, half] = total[:, :COLUMNS].astype(jnp.bfloat16)


def scales(slot_place, refresh, rank, recv):
    smem = pl.BlockSpec(memory_space=pltpu.SMEM)
    return pl.pallas_call(
        scales_kernel,
        in_specs=[smem, smem, smem, pl.BlockSpec(memory_space=pl.ANY)],
        out_specs=pl.BlockSpec(memory_space=pltpu.VMEM),
        out_shape=jax.ShapeDtypeStruct((2, 2, 1, COLUMNS), jnp.bfloat16),
        scratch_shapes=[
            pltpu.VMEM((2, N_TP, SCALE_ROWS, TILE), jnp.bfloat16),
            pltpu.SemaphoreType.DMA((2,)),
        ],
        name="scales",
    )(slot_place, refresh, rank, recv)


def join_kernel(n, bands_ref, *refs):
    pieces, out_ref, buf, sem_in, sem_out = refs[: 2 * n], refs[2 * n], refs[2 * n + 1], refs[2 * n + 2], refs[2 * n + 3]
    fetch = [pltpu.make_async_copy(piece, buf.at[i], sem_in.at[i]) for i, piece in enumerate(pieces)]
    for copy in fetch:
        copy.start()
    store = []
    for i in range(2 * n):
        fetch[i].wait()
        row = pl.multiple_of(bands_ref[i // 2] * BAND, BAND)
        copy = pltpu.make_async_copy(
            buf.at[i], out_ref.at[:, :, pl.ds(row, BAND), pl.ds((i % 2) * PART, PART)], sem_out.at[i]
        )
        copy.start()
        store.append(copy)
    for copy in store:
        copy.wait()


def join(bands, pieces):
    n = len(pieces) // 2
    return pl.pallas_call(
        functools.partial(join_kernel, n),
        in_specs=[pl.BlockSpec(memory_space=pltpu.SMEM)] + [pl.BlockSpec(memory_space=pl.ANY)] * (2 * n),
        out_specs=pl.BlockSpec(memory_space=pl.ANY),
        out_shape=jax.ShapeDtypeStruct((2, 2, TILE, D), jnp.bfloat16),
        scratch_shapes=[
            pltpu.VMEM((2 * n, 2, 2, BAND, PART), jnp.bfloat16),
            pltpu.SemaphoreType.DMA((2 * n,)),
            pltpu.SemaphoreType.DMA((2 * n,)),
        ],
        compiler_params=pltpu.CompilerParams(vmem_limit_bytes=VMEM_LIMIT),
        name="join",
    )(bands, *pieces)


def moves(to):
    return [(4 * x + y, 4 * to(x, y)[0] + to(x, y)[1]) for x in range(2) for y in range(4)]


UP = moves(lambda x, y: (x, (y + 1) % 4))
DOWN = moves(lambda x, y: (x, (y + 3) % 4))
ACROSS = moves(lambda x, y: (1 - x, y))


def gather(a, b):
    up, down, across = (functools.partial(lax.ppermute, axis_name="group", perm=perm) for perm in (UP, DOWN, ACROSS))
    xb = across(b)
    a_prev, a_next = up(a), down(a)
    xa = across(a)
    a_far = up(a_prev)
    b_prev, b_next = up(b), down(b)
    xa_prev = across(a_prev)
    xb_prev, xb_next = up(xb), down(xb)
    xa_next = across(a_next)
    b_far = up(b_prev)
    xb_far = down(xb_next)
    xa_far = across(a_far)
    return [a, b, a_prev, b_prev, a_next, b_next, a_far, b_far, xa, xb, xa_prev, xb_prev, xa_next, xb_next, xa_far, xb_far]


def local(weight_tiles, gradients, momentum, slot_place, refresh):
    group = lax.axis_index("group")
    rank = lax.axis_index("tp").astype(jnp.int32).reshape(1)
    cut = step(weight_tiles[0], gradients[0], momentum[0])
    recv = lax.all_to_all(cut.reshape(N_GROUP * N_TP, ROWS, TILE), ("group", "tp"), 0, 0, tiled=True)
    recv = recv.reshape(N_GROUP, N_TP, ROWS, TILE)
    a, b = place(slot_place, refresh, rank, recv)
    block_scales = scales(slot_place, refresh, rank, recv)
    x, y = group // 4, group % 4
    ys = jnp.stack([y, (y + 3) % 4, (y + 1) % 4, (y + 2) % 4])
    bands = jnp.concatenate([4 * x + ys, 4 * (1 - x) + ys]).astype(jnp.int32)
    slices = join(bands, gather(a, b))
    return (slices[None], block_scales[None])


def solution(mesh):
    placed = (
        P("group", "tp", None, None),
        P("group", "tp", None, None),
        P("group", "tp", None, None),
        P(),
        P(),
    )
    return jax.shard_map(
        local,
        mesh=mesh,
        in_specs=placed,
        out_specs=(P("group", None, None, "tp", None), P("group", None, None, "tp", None)),
        check_vma=False,
    )
```
